32 devices in a mesh: dp: 4 (over z), row: 2 (over y), col: 4 (over x, core).
Axes of the slice: x: 2, y: 2, z: 4, core: 2. Of those that a mesh axis runs over, the one named last changes fastest.
Arguments:
- inputs: bfloat16 [8, 1024, 1024], P('dp', 'col', 'row'), may hold values from -6 to 6
- conditioning: float32 [8, 1024], P('dp', 'col'), may hold values from -6 to 6
- w_mod: bfloat16 [1024, 6, 1024], P('col', None, 'row'), may hold values from -0.1875 to 0.1875
- b_mod: float32 [6, 1024], P(None, 'row'), may hold values from -3 to 3
- w_qkv: bfloat16 [1024, 3, 1024], P('row', None, 'col'), may hold values from -0.1875 to 0.1875
- b_qkv: float32 [2, 1024], P(None, 'col'), may hold values from -3 to 3
- w_out: bfloat16 [1024, 1024], P('col', 'row'), may hold values from -0.75 to 0.75
- b_out: float32 [1024], P('row'), may hold values from -3 to 3
- w_fc1: bfloat16 [1024, 4096], P('row', 'col'), may hold values from -0.1875 to 0.1875
- b_fc1: float32 [4096], P('col'), may hold values from -3 to 3
- w_fc2: bfloat16 [4096, 1024], P('col', 'row'), may hold values from -0.09375 to 0.09375
- b_fc2: float32 [1024], P('row'), may hold values from -3 to 3
- cotangent: bfloat16 [8, 1024, 1024], P('dp', 'col', 'row'), may hold values from -6 to 6
Outputs:
- outputs: float32 [8, 1024, 1024], P('dp', 'col', 'row')
- input_grad: float32 [8, 1024, 1024], P('dp', 'col', 'row')
- cond_grad: float32 [8, 1024], P('dp', 'col')
- grad_mod: float32 [1024, 6, 1024], P('col', None, 'row')
- grad_bmod: float32 [6, 1024], P(None, 'row')
- grad_qkv: float32 [1024, 3, 1024], P('row', None, 'col')
- grad_bqkv: float32 [2, 1024], P(None, 'col')
- grad_out: float32 [1024, 1024], P('col', 'row')
- grad_bout: float32 [1024], P('row')
- grad_fc1: float32 [1024, 4096], P('row', 'col')
- grad_bfc1: float32 [4096], P('col')
- grad_fc2: float32 [4096, 1024], P('col', 'row')
- grad_bfc2: float32 [1024], P('row')
The draws below stay inside these ranges and needn't reach their ends.
All inputs are finite; a program needn't handle non-finite values.
Results may differ from the reference program's by a relative error of at most 0.014.
The reference program's roundings to bfloat16 on the way count: a program that leaves them out, or rounds other values in their place, can miss the bound.
Values may be sent and summed in bfloat16 or wider, within the bound.
A program may use at most 192 MiB of HBM per device.

```python
import jax
import jax.numpy as jnp
from jax import lax

MODEL_WIDTH = 1024
HEADS = 16
HD = 64
FF = 4096
SEQ = 1024
LATENTS = 8


def levels(key, shape, shards, low, top_value):
    loudness, own = 1.0, jax.random.fold_in(key, 6)
    for position, parts in shards:
        heights = jnp.exp(jax.random.uniform(jax.random.fold_in(own, position), (parts,), jnp.float32, low / len(shards), top_value / len(shards)))
        loudness = loudness * jnp.repeat(heights, shape[position] // parts).reshape([-1 if axis == position else 1 for axis in range(len(shape))])
    return loudness


def noise(key, extent, scale, reach, cuts=(), kind=jnp.bfloat16):
    array = jax.random.normal(key, extent, jnp.float32) * scale
    if len(cuts) > 0:
        array = levels(key, extent, cuts, -0.22, 0.18) * array
    return jnp.clip(array, min=-reach, max=reach).astype(kind)


def setup_inputs(seed: int = 0) -> dict:
    splits = jax.random.split(jax.random.key(seed), 14)
    return {
        "inputs": noise(splits[0], (LATENTS, SEQ, MODEL_WIDTH), 1.0, 6.0, ((0, 4), (1, 4), (2, 2))),
        "conditioning": noise(splits[1], (LATENTS, MODEL_WIDTH), 1.0, 6.0, ((0, 4), (1, 4)), jnp.float32),
        "w_mod": noise(splits[2], (MODEL_WIDTH, 6, MODEL_WIDTH), MODEL_WIDTH ** -0.5, 0.1875, ((0, 4), (2, 2))),
        "b_mod": noise(splits[3], (6, MODEL_WIDTH), 0.5, 3.0, ((1, 2),), jnp.float32),
        "w_qkv": noise(splits[4], (MODEL_WIDTH, 3, MODEL_WIDTH), MODEL_WIDTH ** -0.5, 0.1875, ((0, 2), (2, 4))),
        "b_qkv": noise(splits[5], (2, MODEL_WIDTH), 0.5, 3.0, ((1, 4),), jnp.float32),
        "w_out": noise(splits[6], (MODEL_WIDTH, MODEL_WIDTH), (MODEL_WIDTH // 16) ** -0.5, 0.75, ((0, 4), (1, 2))),
        "b_out": noise(splits[7], (MODEL_WIDTH,), 0.5, 3.0, ((0, 2),), jnp.float32),
        "w_fc1": noise(splits[8], (MODEL_WIDTH, FF), MODEL_WIDTH ** -0.5, 0.1875, ((0, 2), (1, 4))),
        "b_fc1": noise(splits[9], (FF,), 0.5, 3.0, ((0, 4),), jnp.float32),
        "w_fc2": noise(splits[10], (FF, MODEL_WIDTH), FF ** -0.5, 0.09375, ((0, 4), (1, 2))),
        "b_fc2": noise(splits[11], (MODEL_WIDTH,), 0.5, 3.0, ((0, 2),), jnp.float32),
        "cotangent": noise(splits[12], (LATENTS, SEQ, MODEL_WIDTH), 1.0, 6.0, ((0, 4), (1, 4), (2, 2))),
    }


def gelu_tanh(value):
    return jax.nn.gelu(value, approximate=True)

def pullback(func, value, upstream_gradient):
    return jax.vjp(func, value)[1](upstream_gradient)[0]

def normalize_rows(value):
    feature_width = value.shape[-1]
    mean = lax.optimization_barrier(jnp.sum(value, -1, keepdims=True)) / feature_width
    var = lax.optimization_barrier(jnp.sum(value * value, -1, keepdims=True)) / feature_width - mean * mean
    inverse_deviation = lax.rsqrt(var + 1e-06)
    return ((value - mean) * inverse_deviation, inverse_deviation)

def layer_norm_backward(normalized_gradient, normalized_input, inverse_deviation):
    feature_width = normalized_gradient.shape[-1]
    first_branch = lax.optimization_barrier(jnp.sum(normalized_gradient, -1, keepdims=True)) / feature_width
    second_branch = lax.optimization_barrier(jnp.sum(normalized_gradient * normalized_input, -1, keepdims=True)) / feature_width
    return inverse_deviation * (normalized_gradient - first_branch - normalized_input * second_branch)

def attend(query, keys, values):
    scores = jnp.einsum('qhd,khd->hqk', query.astype(jnp.float32), keys.astype(jnp.float32)) * HD ** (-0.5)
    top = lax.optimization_barrier(jnp.max(scores, -1, keepdims=True))
    expd = jnp.exp(scores - top)
    total = lax.optimization_barrier(jnp.sum(expd, -1, keepdims=True))
    probs = (expd / total).astype(jnp.bfloat16)
    out = jnp.einsum('hqk,khd->qhd', probs.astype(jnp.float32), values.astype(jnp.float32)).astype(jnp.bfloat16)
    return (out, top[..., 0] + jnp.log(total[..., 0]))

def attend_back(query, keys, values, lse, dattended):
    scores = jnp.einsum('qhd,khd->hqk', query.astype(jnp.float32), keys.astype(jnp.float32)) * HD ** (-0.5)
    probs = jnp.exp(scores - lse[..., None])
    probs_b = probs.astype(jnp.bfloat16).astype(jnp.float32)
    dfl = dattended.astype(jnp.float32)
    dvalues = jnp.einsum('hqk,qhd->khd', probs_b, dfl)
    dprobs = jnp.einsum('qhd,khd->hqk', dfl, values.astype(jnp.float32))
    delta = lax.optimization_barrier(jnp.sum(probs * dprobs, -1, keepdims=True))
    dscores = (probs * (dprobs - delta) * HD ** (-0.5)).astype(jnp.bfloat16).astype(jnp.float32)
    dquery = jnp.einsum('hqk,khd->qhd', dscores, keys.astype(jnp.float32))
    dkeys = jnp.einsum('hqk,qhd->khd', dscores, query.astype(jnp.float32))
    return (dquery, dkeys, dvalues)

def one_latent(params, tokens, cond, cotan):
    w_mod, b_mod, w_qkv, b_qkv, w_out, b_out, w_fc1, b_fc1, w_fc2, b_fc2 = params
    f32 = jnp.float32
    brain_float_sixteen = jnp.bfloat16
    input_single_precision = tokens.astype(f32)
    cond_act = jax.nn.silu(cond).astype(brain_float_sixteen)
    modulation_rows = jnp.dot(cond_act[None, :], w_mod.reshape(MODEL_WIDTH, 6 * MODEL_WIDTH), preferred_element_type=f32).reshape(6, MODEL_WIDTH) + b_mod
    first_normalized_input, first_inverse_deviation = normalize_rows(input_single_precision)
    first_hidden_state = (first_normalized_input * (1.0 + modulation_rows[1]) + modulation_rows[0]).astype(brain_float_sixteen)
    qkv = jnp.dot(first_hidden_state, w_qkv.reshape(MODEL_WIDTH, 3 * MODEL_WIDTH), preferred_element_type=f32).reshape(SEQ, 3, MODEL_WIDTH)
    query = (qkv[:, 0] + b_qkv[0]).astype(brain_float_sixteen)
    keys = qkv[:, 1].astype(brain_float_sixteen)
    values = (qkv[:, 2] + b_qkv[1]).astype(brain_float_sixteen)
    q3 = query.reshape(SEQ, HEADS, HD)
    k3 = keys.reshape(SEQ, HEADS, HD)
    v3 = values.reshape(SEQ, HEADS, HD)
    attended, lse = attend(q3, k3, v3)
    attended = attended.reshape(SEQ, MODEL_WIDTH)
    projected = jnp.dot(attended, w_out, preferred_element_type=f32) + b_out
    midpoint_state = input_single_precision + modulation_rows[2] * projected
    second_normalized_input, second_inverse_deviation = normalize_rows(midpoint_state)
    second_hidden_state = (second_normalized_input * (1.0 + modulation_rows[4]) + modulation_rows[3]).astype(brain_float_sixteen)
    pre = jnp.dot(second_hidden_state, w_fc1, preferred_element_type=f32) + b_fc1
    hidden = gelu_tanh(pre).astype(brain_float_sixteen)
    feed = jnp.dot(hidden, w_fc2, preferred_element_type=f32) + b_fc2
    result = midpoint_state + modulation_rows[5] * feed
    upstream_gradient = cotan.astype(f32)
    dgate2 = lax.optimization_barrier(jnp.sum(upstream_gradient * feed, 0))
    dfeed = upstream_gradient * modulation_rows[5]
    dfeed_b = dfeed.astype(brain_float_sixteen)
    g_fc2 = jnp.dot(hidden.T, dfeed_b, preferred_element_type=f32)
    g_bfc2 = lax.optimization_barrier(jnp.sum(dfeed, 0))
    dhidden = jnp.dot(dfeed_b, w_fc2.T, preferred_element_type=f32)
    dpre = pullback(gelu_tanh, pre, dhidden)
    dpre_b = dpre.astype(brain_float_sixteen)
    g_fc1 = jnp.dot(second_hidden_state.T, dpre_b, preferred_element_type=f32)
    g_bfc1 = lax.optimization_barrier(jnp.sum(dpre, 0))
    second_hidden_gradient = jnp.dot(dpre_b, w_fc1.T, preferred_element_type=f32)
    second_scale_gradient = lax.optimization_barrier(jnp.sum(second_hidden_gradient * second_normalized_input, 0))
    dshift2 = lax.optimization_barrier(jnp.sum(second_hidden_gradient, 0))
    midpoint_gradient = upstream_gradient + layer_norm_backward(second_hidden_gradient * (1.0 + modulation_rows[4]), second_normalized_input, second_inverse_deviation)
    dgate1 = lax.optimization_barrier(jnp.sum(midpoint_gradient * projected, 0))
    dproj = midpoint_gradient * modulation_rows[2]
    dproj_b = dproj.astype(brain_float_sixteen)
    g_out = jnp.dot(attended.T, dproj_b, preferred_element_type=f32)
    g_bout = lax.optimization_barrier(jnp.sum(dproj, 0))
    dattended = jnp.dot(dproj_b, w_out.T, preferred_element_type=f32).astype(brain_float_sixteen)
    dquery, dkeys, dvalues = attend_back(q3, k3, v3, lse, dattended.reshape(SEQ, HEADS, HD))
    dquery = dquery.reshape(SEQ, MODEL_WIDTH)
    dkeys = dkeys.reshape(SEQ, MODEL_WIDTH)
    dvalues = dvalues.reshape(SEQ, MODEL_WIDTH)
    g_bqkv = jnp.stack([lax.optimization_barrier(jnp.sum(dquery, 0)), lax.optimization_barrier(jnp.sum(dvalues, 0))])
    dqkv = jnp.stack([dquery, dkeys, dvalues], 1).astype(brain_float_sixteen).reshape(SEQ, 3 * MODEL_WIDTH)
    g_qkv = jnp.dot(first_hidden_state.T, dqkv, preferred_element_type=f32).reshape(MODEL_WIDTH, 3, MODEL_WIDTH)
    first_hidden_gradient = jnp.dot(dqkv, w_qkv.reshape(MODEL_WIDTH, 3 * MODEL_WIDTH).T, preferred_element_type=f32)
    first_scale_gradient = lax.optimization_barrier(jnp.sum(first_hidden_gradient * first_normalized_input, 0))
    dshift1 = lax.optimization_barrier(jnp.sum(first_hidden_gradient, 0))
    gradient_of_input = midpoint_gradient + layer_norm_backward(first_hidden_gradient * (1.0 + modulation_rows[1]), first_normalized_input, first_inverse_deviation)
    dmod = jnp.stack([dshift1, first_scale_gradient, dgate1, dshift2, second_scale_gradient, dgate2])
    dmod_b = dmod.astype(brain_float_sixteen).reshape(1, 6 * MODEL_WIDTH)
    g_mod = jnp.dot(cond_act[:, None], dmod_b, preferred_element_type=f32).reshape(MODEL_WIDTH, 6, MODEL_WIDTH)
    dcond_act = jnp.dot(dmod_b, w_mod.reshape(MODEL_WIDTH, 6 * MODEL_WIDTH).T, preferred_element_type=f32)[0]
    dcond = pullback(jax.nn.silu, cond, dcond_act)
    grads = (g_mod, dmod, g_qkv, g_bqkv, g_out, g_bout, g_fc1, g_bfc1, g_fc2, g_bfc2)
    return (result, gradient_of_input, dcond, grads)

def reference(inputs, conditioning, w_mod, b_mod, w_qkv, b_qkv, w_out, b_out, w_fc1, b_fc1, w_fc2, b_fc2, cotangent):
    params = (w_mod, b_mod, w_qkv, b_qkv, w_out, b_out, w_fc1, b_fc1, w_fc2, b_fc2)
    zeros = (jnp.zeros((MODEL_WIDTH, 6, MODEL_WIDTH), jnp.float32), jnp.zeros((6, MODEL_WIDTH), jnp.float32), jnp.zeros((MODEL_WIDTH, 3, MODEL_WIDTH), jnp.float32), jnp.zeros((2, MODEL_WIDTH), jnp.float32), jnp.zeros((MODEL_WIDTH, MODEL_WIDTH), jnp.float32), jnp.zeros((MODEL_WIDTH,), jnp.float32), jnp.zeros((MODEL_WIDTH, FF), jnp.float32), jnp.zeros((FF,), jnp.float32), jnp.zeros((FF, MODEL_WIDTH), jnp.float32), jnp.zeros((MODEL_WIDTH,), jnp.float32))

    def step(carry, item):
        tokens, cond, cotan = item
        result, gradient_of_input, dcond, grads = one_latent(params, tokens, cond, cotan)
        carry = tuple((a + b for a, b in zip(carry, grads)))
        return (carry, (result, gradient_of_input, dcond))
    totals, (results, dinputs, dconds) = lax.scan(step, zeros, (inputs, conditioning, cotangent))
    g_mod, g_bmod, g_qkv, g_bqkv, g_out, g_bout, g_fc1, g_bfc1, g_fc2, g_bfc2 = totals
    return (results, dinputs, dconds, g_mod, g_bmod, g_qkv, g_bqkv, g_out, g_bout, g_fc1, g_bfc1, g_fc2, g_bfc2)
```

```python
import jax
import jax.numpy as jnp
from jax import lax
from jax.experimental import pallas as pl
from jax.experimental.pallas import tpu as pltpu
from jax.sharding import PartitionSpec as P

MODEL_WIDTH = 1024
HD = 64


def gelu_tanh(value):
    return jax.nn.gelu(value, approximate=True)


def pullback(func, value, upstream_gradient):
    return jax.vjp(func, value)[1](upstream_gradient)[0]


def rows_gather(active):
    return lax.all_gather(active, "row", axis=1, tiled=True)


def rows_sum(partial_value):
    return lax.psum_scatter(partial_value, "row", scatter_dimension=1, tiled=True)


def cols_gather(active):
    return lax.all_gather(active, "col", axis=1, tiled=True)


def cols_sum(partial_value):
    return lax.psum_scatter(partial_value, "col", scatter_dimension=1, tiled=True)


def summed_per_row(first_branch, second_branch):
    return lax.psum((first_branch, second_branch), "row")


def sharded_layer_norm(value):
    total, squares = summed_per_row(jnp.sum(value, -1), jnp.sum(value * value, -1))
    mean = (total / MODEL_WIDTH)[..., None]
    var = (squares / MODEL_WIDTH)[..., None] - mean * mean
    inverse_deviation = lax.rsqrt(var + 1e-06)
    return ((value - mean) * inverse_deviation, inverse_deviation)


def sharded_layer_norm_backward(normalized_gradient, normalized_input, inverse_deviation):
    first_branch, second_branch = summed_per_row(
        jnp.sum(normalized_gradient, -1), jnp.sum(normalized_gradient * normalized_input, -1)
    )
    return inverse_deviation * (
        normalized_gradient
        - (first_branch / MODEL_WIDTH)[..., None]
        - normalized_input * (second_branch / MODEL_WIDTH)[..., None]
    )


def modulate(cond_act, w_mod, b_mod):
    part = jnp.einsum("ld,dke->lke", cond_act, w_mod, preferred_element_type=jnp.float32)
    return lax.psum(part, "col") + b_mod


def pieces(modulation_rows):
    return tuple((modulation_rows[:, number][:, None, :] for number in range(6)))


def split_qkv(qkv, b_qkv):
    query = (qkv[:, :, 0] + b_qkv[0]).astype(jnp.bfloat16)
    keys_vals = jnp.concatenate([qkv[:, :, 1], qkv[:, :, 2] + b_qkv[1]], 2).astype(jnp.bfloat16)
    return (query, keys_vals)


def attend_one(item):
    query, keys, values = item
    scores = jnp.einsum("qhd,khd->hqk", query, keys, preferred_element_type=jnp.float32) * HD ** (
        -0.5
    )
    top = jnp.max(scores, -1, keepdims=True)
    expd = jnp.exp(scores - top)
    total = jnp.sum(expd, -1, keepdims=True)
    probs = (expd / total).astype(jnp.bfloat16)
    out = jnp.einsum("hqk,khd->qhd", probs, values, preferred_element_type=jnp.float32).astype(
        jnp.bfloat16
    )
    return (out, top[..., 0] + jnp.log(total[..., 0]))


def attend_back_one(item):
    query, keys, values, lse, dattended = item
    scores = jnp.einsum("qhd,khd->hqk", query, keys, preferred_element_type=jnp.float32) * HD ** (
        -0.5
    )
    probs = jnp.exp(scores - lse[..., None])
    probs_b = probs.astype(jnp.bfloat16)
    dvalues = jnp.einsum("hqk,qhd->khd", probs_b, dattended, preferred_element_type=jnp.float32)
    dprobs = jnp.einsum("qhd,khd->hqk", dattended, values, preferred_element_type=jnp.float32)
    delta = jnp.sum(probs * dprobs, -1, keepdims=True)
    dscores = (probs * (dprobs - delta) * HD ** (-0.5)).astype(jnp.bfloat16)
    dquery = jnp.einsum("hqk,khd->qhd", dscores, keys, preferred_element_type=jnp.float32)
    dkeys = jnp.einsum("hqk,qhd->khd", dscores, query, preferred_element_type=jnp.float32)
    return (dquery, dkeys, dvalues)


def attention(query, keys_vals):
    latents, seq_rows, feature_width = query.shape
    head_cols = feature_width // HD
    kv_all = rows_gather(keys_vals)
    seq_all = kv_all.shape[1]
    q_four = query.reshape(latents, seq_rows, head_cols, HD)
    k_four = kv_all[:, :, :feature_width].reshape(latents, seq_all, head_cols, HD)
    v_four = kv_all[:, :, feature_width:].reshape(latents, seq_all, head_cols, HD)
    attended, lse = lax.map(attend_one, (q_four, k_four, v_four))
    return (attended.reshape(latents, seq_rows, feature_width), (q_four, k_four, v_four, lse))


def attention_back(saved, dattended):
    q_four, k_four, v_four, lse = saved
    latents, seq_rows, head_cols, _ = q_four.shape
    feature_width = head_cols * HD
    seq_all = k_four.shape[1]
    datt_four = dattended.reshape(latents, seq_rows, head_cols, HD)
    dquery, dkeys, dvalues = lax.map(attend_back_one, (q_four, k_four, v_four, lse, datt_four))
    dkv_part = jnp.concatenate(
        [
            dkeys.reshape(latents, seq_all, feature_width),
            dvalues.reshape(latents, seq_all, feature_width),
        ],
        2,
    )
    dkv = rows_sum(dkv_part)
    dquery = dquery.reshape(latents, seq_rows, feature_width)
    bqkv_part = jnp.stack([jnp.sum(dquery, (0, 1)), jnp.sum(dkv[:, :, feature_width:], (0, 1))])
    dqkv = jnp.concatenate(
        [dquery[:, :, None, :], dkv.reshape(latents, seq_rows, 2, feature_width)], 2
    ).astype(jnp.bfloat16)
    return (bqkv_part, dqkv)


def run_blocks(
    inputs, modulation_rows, w_qkv, b_qkv, w_out, b_out, w_fc1, b_fc1, w_fc2, b_fc2, cotangent
):
    f32 = jnp.float32
    brain_float_sixteen = jnp.bfloat16
    first_offset, first_scale, gate1, second_offset, second_scale, gate2 = pieces(modulation_rows)
    input_single_precision = inputs.astype(f32)
    first_normalized_input, first_inverse_deviation = sharded_layer_norm(input_single_precision)
    first_hidden_state = (first_normalized_input * (1.0 + first_scale) + first_offset).astype(
        brain_float_sixteen
    )
    h_one_all = cols_gather(first_hidden_state)
    qkv = rows_sum(jnp.einsum("lsd,dke->lske", h_one_all, w_qkv, preferred_element_type=f32))
    query, keys_vals = split_qkv(qkv, b_qkv)
    attended, saved = attention(query, keys_vals)
    att_all = rows_gather(attended)
    projected = (
        cols_sum(jnp.einsum("lsh,he->lse", att_all, w_out, preferred_element_type=f32)) + b_out
    )
    midpoint_state = input_single_precision + gate1 * projected
    second_normalized_input, second_inverse_deviation = sharded_layer_norm(midpoint_state)
    second_hidden_state = (second_normalized_input * (1.0 + second_scale) + second_offset).astype(
        brain_float_sixteen
    )
    h_two_all = cols_gather(second_hidden_state)
    pre = rows_sum(jnp.einsum("lsd,dh->lsh", h_two_all, w_fc1, preferred_element_type=f32)) + b_fc1
    hidden = gelu_tanh(pre).astype(brain_float_sixteen)
    hidden_all = rows_gather(hidden)
    feed = (
        cols_sum(jnp.einsum("lsh,hd->lsd", hidden_all, w_fc2, preferred_element_type=f32)) + b_fc2
    )
    result = midpoint_state + gate2 * feed
    upstream_gradient = cotangent.astype(f32)
    dgate2 = jnp.sum(upstream_gradient * feed, 1)
    dfeed = upstream_gradient * gate2
    bfc2_part = jnp.sum(dfeed, (0, 1))
    dfeed_all = cols_gather(dfeed.astype(brain_float_sixteen))
    dhidden = rows_sum(jnp.einsum("lsd,hd->lsh", dfeed_all, w_fc2, preferred_element_type=f32))
    g_fc2 = jnp.einsum("lsh,lsd->hd", hidden_all, dfeed_all, preferred_element_type=f32)
    dpre = pullback(gelu_tanh, pre, dhidden)
    bfc1_part = jnp.sum(dpre, (0, 1))
    dpre_all = rows_gather(dpre.astype(brain_float_sixteen))
    second_hidden_gradient = cols_sum(
        jnp.einsum("lsh,dh->lsd", dpre_all, w_fc1, preferred_element_type=f32)
    )
    g_fc1 = jnp.einsum("lsd,lsh->dh", h_two_all, dpre_all, preferred_element_type=f32)
    second_scale_gradient = jnp.sum(second_hidden_gradient * second_normalized_input, 1)
    dshift2 = jnp.sum(second_hidden_gradient, 1)
    midpoint_gradient = upstream_gradient + sharded_layer_norm_backward(
        second_hidden_gradient * (1.0 + second_scale),
        second_normalized_input,
        second_inverse_deviation,
    )
    dgate1 = jnp.sum(midpoint_gradient * projected, 1)
    dproj = midpoint_gradient * gate1
    bout_part = jnp.sum(dproj, (0, 1))
    dproj_all = cols_gather(dproj.astype(brain_float_sixteen))
    dattended = rows_sum(
        jnp.einsum("lsd,hd->lsh", dproj_all, w_out, preferred_element_type=f32)
    ).astype(brain_float_sixteen)
    g_out = jnp.einsum("lsh,lsd->hd", att_all, dproj_all, preferred_element_type=f32)
    bqkv_part, dqkv = attention_back(saved, dattended)
    dqkv_all = rows_gather(dqkv)
    first_hidden_gradient = cols_sum(
        jnp.einsum("lske,dke->lsd", dqkv_all, w_qkv, preferred_element_type=f32)
    )
    g_qkv = jnp.einsum("lsd,lske->dke", h_one_all, dqkv_all, preferred_element_type=f32)
    first_scale_gradient = jnp.sum(first_hidden_gradient * first_normalized_input, 1)
    dshift1 = jnp.sum(first_hidden_gradient, 1)
    gradient_of_input = midpoint_gradient + sharded_layer_norm_backward(
        first_hidden_gradient * (1.0 + first_scale), first_normalized_input, first_inverse_deviation
    )
    dmod_part = jnp.stack(
        [dshift1, first_scale_gradient, dgate1, dshift2, second_scale_gradient, dgate2], 1
    )
    return (
        result,
        gradient_of_input,
        (dmod_part, bout_part, bfc2_part),
        bfc1_part,
        bqkv_part,
        (g_qkv, g_out, g_fc1, g_fc2),
    )


def finish(conditioning, cond_act, w_mod, resid_parts, bfc1_part, bqkv_part, weight_grads):
    f32 = jnp.float32
    dmod_part, bout_part, bfc2_part = resid_parts
    g_qkv, g_out, g_fc1, g_fc2 = weight_grads
    dmod, g_bout, g_bfc2 = lax.psum((dmod_part, bout_part, bfc2_part), "col")
    dmod_b = dmod.astype(jnp.bfloat16)
    g_mod = jnp.einsum("ld,lke->dke", cond_act, dmod_b, preferred_element_type=f32)
    g_bmod = jnp.sum(dmod, 0)
    dcond_part = jnp.einsum("lke,dke->ld", dmod_b, w_mod, preferred_element_type=f32)
    dcond_act, g_bfc1, g_bqkv = lax.psum((dcond_part, bfc1_part, bqkv_part), "row")
    dcond = pullback(jax.nn.silu, conditioning, dcond_act)
    totals = (
        lax.psum(g_mod.astype(jnp.bfloat16), "dp").astype(jnp.float32),
        lax.psum(g_bmod.astype(jnp.bfloat16), "dp").astype(jnp.float32),
        lax.psum(g_qkv.astype(jnp.bfloat16), "dp").astype(jnp.float32),
        lax.psum(g_bqkv.astype(jnp.bfloat16), "dp").astype(jnp.float32),
        lax.psum(g_out.astype(jnp.bfloat16), "dp").astype(jnp.float32),
        lax.psum(g_bout.astype(jnp.bfloat16), "dp").astype(jnp.float32),
        lax.psum(g_fc1.astype(jnp.bfloat16), "dp").astype(jnp.float32),
        lax.psum(g_bfc1.astype(jnp.bfloat16), "dp").astype(jnp.float32),
        lax.psum(g_fc2.astype(jnp.bfloat16), "dp").astype(jnp.float32),
        lax.psum(g_bfc2.astype(jnp.bfloat16), "dp").astype(jnp.float32),
    )
    return (dcond, totals)


INTERPRET = False


def kernel_probs(query, keys, first, head):
    mask = (first >= head * HD) & (first < (head + 1) * HD)
    picked = jnp.where(mask, query, jnp.zeros_like(query))
    scores = lax.dot_general(
        keys, picked, (((1,), (1,)), ((), ())), preferred_element_type=jnp.float32
    ) * HD ** (-0.5)
    top = jnp.max(scores, 0, keepdims=True)
    expd = jnp.exp(scores - top)
    return (mask, expd / jnp.sum(expd, 0, keepdims=True))


def forward_kernel(q_ref, k_ref, v_ref, o_ref):
    query, keys, values = (q_ref[...], k_ref[...], v_ref[...])
    lanes = lax.broadcasted_iota(jnp.int32, query.shape, 1)
    total = jnp.zeros(query.shape, jnp.float32)
    for head in range(query.shape[1] // HD):
        mask, probs = kernel_probs(query, keys, lanes, head)
        part = lax.dot_general(
            probs.astype(jnp.bfloat16),
            values,
            (((0,), (0,)), ((), ())),
            preferred_element_type=jnp.float32,
        )
        total = jnp.where(mask, part, total)
    o_ref[...] = total.astype(jnp.bfloat16)


def backward_kernel(q_ref, k_ref, v_ref, do_ref, dq_ref, dk_ref, dv_ref):
    query, keys, values, upstream = (q_ref[...], k_ref[...], v_ref[...], do_ref[...])
    lanes = lax.broadcasted_iota(jnp.int32, query.shape, 1)

    @pl.when(pl.program_id(1) == 0)
    def _():
        dk_ref[...] = jnp.zeros_like(dk_ref)
        dv_ref[...] = jnp.zeros_like(dv_ref)

    total = jnp.zeros(query.shape, jnp.float32)
    for head in range(query.shape[1] // HD):
        mask, probs = kernel_probs(query, keys, lanes, head)
        up_head = jnp.where(mask, upstream, jnp.zeros_like(upstream))
        q_head = jnp.where(mask, query, jnp.zeros_like(query))
        dv_ref[...] += jnp.dot(
            probs.astype(jnp.bfloat16), up_head, preferred_element_type=jnp.float32
        )
        dprobs = lax.dot_general(
            values, up_head, (((1,), (1,)), ((), ())), preferred_element_type=jnp.float32
        )
        delta = jnp.sum(probs * dprobs, 0, keepdims=True)
        dscores = (probs * (dprobs - delta) * HD ** (-0.5)).astype(jnp.bfloat16)
        dk_ref[...] += jnp.dot(dscores, q_head, preferred_element_type=jnp.float32)
        part = lax.dot_general(
            dscores, keys, (((0,), (0,)), ((), ())), preferred_element_type=jnp.float32
        )
        total = jnp.where(mask, part, total)
    dq_ref[...] = total


def attention_specs(latents, seq, width):
    block = min(seq, 256)
    rows = pl.BlockSpec((None, block, width), lambda i, j: (i, j, 0))
    whole = pl.BlockSpec((None, seq, width), lambda i, j: (i, 0, 0))
    return ((latents, seq // block), rows, whole)


def attend_forward(query, keys, values):
    grid, rows, whole = attention_specs(*query.shape)
    return pl.pallas_call(
        forward_kernel,
        grid=grid,
        in_specs=[rows, whole, whole],
        out_specs=rows,
        out_shape=jax.ShapeDtypeStruct(query.shape, jnp.bfloat16),
        interpret=INTERPRET,
    )(query, keys, values)


def attend_backward(query, keys, values, upstream):
    grid, rows, whole = attention_specs(*query.shape)
    shape = jax.ShapeDtypeStruct(query.shape, jnp.float32)
    return pl.pallas_call(
        backward_kernel,
        grid=grid,
        in_specs=[rows, whole, whole, rows],
        out_specs=[rows, whole, whole],
        out_shape=[shape, shape, shape],
        interpret=INTERPRET,
    )(query, keys, values, upstream)


def swap(value, axis, size, distance):
    return lax.ppermute(value, axis, [(i, i ^ distance) for i in range(size)])


def row_swap(value):
    return swap(value, "row", 2, 1)


def near_swap(value):
    return swap(value, "col", 4, 1)


def far_swap(value):
    return swap(value, "col", 4, 2)


def tokens_gather(own):
    far = far_swap(own)
    near = near_swap(own)
    return jnp.concatenate([own, near, far, near_swap(far)], 1)


def tokens_sum(part):
    bf16, f32 = (jnp.bfloat16, jnp.float32)
    latents, tokens, width = part.shape
    four = part.reshape(latents, 4, tokens // 4, width)
    from_near_far = near_swap(four[:, 3].astype(bf16))
    from_near = near_swap(four[:, 1].astype(bf16))
    from_far = far_swap((four[:, 2] + from_near_far.astype(f32)).astype(bf16))
    return four[:, 0] + from_near.astype(f32) + from_far.astype(f32)


def col_total(value):
    value = value + near_swap(value)
    return value + far_swap(value)


def with_peer(own, axis):
    return jnp.concatenate([own, row_swap(own)], axis)


def row_reduced(part, axis):
    own, other = jnp.split(part, 2, axis)
    return own + row_swap(other.astype(jnp.bfloat16)).astype(jnp.float32)


def dp_vector_total(value, size):
    distance = 1
    while distance < size:
        value = value + swap(value, "dp", size, distance)
        distance *= 2
    return value


def dp_ordered(value, size):
    index = lax.axis_index("dp")
    full = jnp.zeros((size,) + value.shape, value.dtype)
    for distance in range(size):
        piece = swap(value, "dp", size, distance) if distance else value
        full = lax.dynamic_update_slice(
            full, piece[None], (index ^ distance,) + (0,) * value.ndim
        )
    return full.reshape((size * value.shape[0],) + value.shape[1:])


def ordered(bit, own, other):
    return jnp.where(
        bit == 0, jnp.concatenate([own, other], 0), jnp.concatenate([other, own], 0)
    )


def dp_matrix_total(value, size):
    index = lax.axis_index("dp")
    bits = []
    distance = 1
    while distance < size:
        bit = (index // distance) % 2
        half = value.shape[0] // 2
        keep = lax.dynamic_slice_in_dim(value, bit * half, half, 0)
        give = lax.dynamic_slice_in_dim(value, (1 - bit) * half, half, 0)
        value = keep + swap(give.astype(jnp.bfloat16), "dp", size, distance).astype(jnp.float32)
        bits.append((bit, distance))
        distance *= 2
    value = value.astype(jnp.bfloat16)
    for bit, distance in reversed(bits):
        value = ordered(bit, value, swap(value, "dp", size, distance))
    return value.astype(jnp.float32)


def full_norm(value):
    mean = jnp.mean(value, -1, keepdims=True)
    var = jnp.mean(value * value, -1, keepdims=True) - mean * mean
    inverse = lax.rsqrt(var + 1e-06)
    return ((value - mean) * inverse, inverse)


def full_norm_back(upstream, normal, inverse):
    return inverse * (
        upstream
        - jnp.mean(upstream, -1, keepdims=True)
        - normal * jnp.mean(upstream * normal, -1, keepdims=True)
    )


def on_device_by_latent(dp_size):
    def run(
        inputs,
        conditioning,
        w_mod,
        b_mod,
        w_qkv,
        b_qkv,
        w_out,
        b_out,
        w_fc1,
        b_fc1,
        w_fc2,
        b_fc2,
        cotangent,
    ):
        f32, bf16 = (jnp.float32, jnp.bfloat16)
        row = lax.axis_index("row")
        latents, tokens, half = inputs.shape
        mine = latents // 2
        width = w_qkv.shape[2]

        def latent_exchange(value):
            own = lax.dynamic_slice_in_dim(value, row * mine, mine, 0)
            other = lax.dynamic_slice_in_dim(value, (1 - row) * mine, mine, 0)
            return jnp.concatenate([own, row_swap(other)], -1)

        def latent_return(value, kind):
            back = row_swap(value[..., half:].astype(kind)).astype(f32)
            return ordered(row, value[..., :half], back)

        def mm(left, right, lc, rc):
            return lax.dot_general(
                left, right, (((lc,), (rc,)), ((), ())), preferred_element_type=f32
            )

        def flat(value):
            return value.reshape(-1, value.shape[-1])

        x_own = latent_exchange(inputs)
        x_all = tokens_gather(x_own)
        cond_act = jax.nn.silu(conditioning).astype(bf16)
        mod_part = jnp.einsum("ld,dke->lke", cond_act, w_mod, preferred_element_type=f32)
        mod_part = latent_exchange(mod_part)
        bias_peer = row_swap(jnp.concatenate([b_mod, b_out[None], b_fc2[None]], 0))
        modulation = col_total(mod_part) + jnp.concatenate([b_mod, bias_peer[:6]], 1)
        out_bias = jnp.concatenate([b_out, bias_peer[6]])
        fc2_bias = jnp.concatenate([b_fc2, bias_peer[7]])
        shift1, scale1, gate1, shift2, scale2, gate2 = pieces(modulation)
        qkv_w = with_peer(w_qkv.reshape(half, 3 * width), 0)
        g_own = latent_exchange(cotangent)
        out_w = with_peer(w_out, 1)
        g_all = tokens_gather(g_own)
        fc2_w = with_peer(w_fc2, 1)
        fc1_w = with_peer(w_fc1, 0)

        hat_all, _ = full_norm(x_all.astype(f32))
        h1_all = flat((hat_all * (1.0 + scale1) + shift1).astype(bf16))
        seq = x_all.shape[1]
        qkv_bias = jnp.concatenate([b_qkv[0], jnp.zeros((width,), f32), b_qkv[1]])
        qkv = (mm(h1_all, qkv_w, 1, 0) + qkv_bias).astype(bf16).reshape(mine, seq, 3 * width)
        query, keys, values = jnp.split(qkv, 3, 2)
        att_all = attend_forward(query, keys, values)
        att_flat = flat(att_all)
        projected = tokens_sum(mm(att_flat, out_w, 1, 0).reshape(mine, seq, -1)) + out_bias
        x_single = x_own.astype(f32)
        mid = x_single + gate1 * projected
        hat2, inverse2 = full_norm(mid)
        h2_all = flat(tokens_gather((hat2 * (1.0 + scale2) + shift2).astype(bf16)))

        upstream = g_own.astype(f32)
        dfeed_all = flat((g_all.astype(f32) * gate2).astype(bf16))
        dhidden = mm(dfeed_all, fc2_w, 1, 1)
        pre = mm(h2_all, fc1_w, 1, 0) + b_fc1
        hidden = gelu_tanh(pre).astype(bf16)
        dpre = pullback(gelu_tanh, pre, dhidden)
        bfc1_part = jnp.sum(dpre, 0)
        dpre_b = dpre.astype(bf16)
        dh2 = tokens_sum(mm(dpre_b, fc1_w, 1, 1).reshape(mine, seq, -1))
        g_fc1 = row_reduced(mm(h2_all, dpre_b, 0, 0), 0)
        g_fc2 = row_reduced(mm(hidden, dfeed_all, 0, 0), 1)
        feed = tokens_sum(mm(hidden, fc2_w, 1, 0).reshape(mine, seq, -1)) + fc2_bias
        result = latent_return(mid + gate2 * feed, f32)
        dgate2 = jnp.sum(upstream * feed, 1)
        bfc2_part = jnp.sum(upstream * gate2, (0, 1))

        dscale2 = jnp.sum(dh2 * hat2, 1)
        dshift2 = jnp.sum(dh2, 1)
        dmid = upstream + full_norm_back(dh2 * (1.0 + scale2), hat2, inverse2)
        dgate1 = jnp.sum(dmid * projected, 1)
        dproj = dmid * gate1
        bout_part = jnp.sum(dproj, (0, 1))
        dproj_all = flat(tokens_gather(dproj.astype(bf16)))
        datt = mm(dproj_all, out_w, 1, 1).astype(bf16).reshape(mine, seq, width)
        g_out = row_reduced(mm(att_flat, dproj_all, 0, 0), 1)
        dquery, dkeys, dvalues = attend_backward(query, keys, values, datt)
        bqkv_part = jnp.stack([jnp.sum(dquery, (0, 1)), jnp.sum(dvalues, (0, 1))])
        dqkv = flat(jnp.concatenate([dquery, dkeys, dvalues], 2).astype(bf16))
        dh1 = tokens_sum(mm(dqkv, qkv_w, 1, 1).reshape(mine, seq, -1))
        g_qkv = row_reduced(mm(h1_all, dqkv, 0, 0), 0)

        hat1, inverse1 = full_norm(x_single)
        dscale1 = jnp.sum(dh1 * hat1, 1)
        dshift1 = jnp.sum(dh1, 1)
        x_grad = dmid + full_norm_back(dh1 * (1.0 + scale1), hat1, inverse1)
        gradient_of_input = latent_return(x_grad, bf16)

        vectors = jnp.concatenate(
            [
                jnp.stack([dshift1, dscale1, dgate1, dshift2, dscale2, dgate2], 1).reshape(
                    6 * mine, 2 * half
                ),
                bout_part[None],
                bfc2_part[None],
            ],
            0,
        )
        vectors = col_total(vectors)
        v_own, v_recv = (vectors[:, :half], row_swap(vectors[:, half:]))
        dmod = ordered(
            row,
            v_own[: 6 * mine].reshape(mine, 6, half),
            v_recv[: 6 * mine].reshape(mine, 6, half),
        )
        dmod_b = dmod.astype(bf16)
        dcond_part = jnp.einsum("lke,dke->ld", dmod_b, w_mod, preferred_element_type=f32)
        hidden_side = jnp.concatenate([bfc1_part, bqkv_part.reshape(-1)])
        hidden_side = hidden_side + row_swap(hidden_side)
        dcond = pullback(jax.nn.silu, conditioning, dcond_part + row_swap(dcond_part))
        resid_side = (v_own + v_recv)[6 * mine :]
        cond_every = dp_ordered(cond_act, dp_size)
        dmod_every = dp_ordered(dmod_b, dp_size)
        g_mod = jnp.einsum("ld,lke->dke", cond_every, dmod_every, preferred_element_type=f32)
        sums = dp_vector_total(
            jnp.concatenate([jnp.sum(dmod, 0).reshape(-1), resid_side.reshape(-1), hidden_side]),
            dp_size,
        )
        g_bmod = sums[: 6 * half].reshape(6, half)
        g_bout = sums[6 * half : 7 * half]
        g_bfc2 = sums[7 * half : 8 * half]
        g_bfc1 = sums[8 * half : 8 * half + bfc1_part.shape[0]]
        g_bqkv = sums[8 * half + bfc1_part.shape[0] :].reshape(2, width)
        return (
            result,
            gradient_of_input,
            dcond,
            g_mod,
            g_bmod,
            dp_matrix_total(g_qkv, dp_size).reshape(half, 3, width),
            g_bqkv,
            dp_matrix_total(g_out, dp_size),
            g_bout,
            dp_matrix_total(g_fc1, dp_size),
            g_bfc1,
            dp_matrix_total(g_fc2, dp_size),
            g_bfc2,
        )

    return run


def fits_by_latent(mesh):
    size = mesh.shape["dp"]
    return mesh.shape["row"] == 2 and mesh.shape["col"] == 4 and size & (size - 1) == 0


def on_device(
    inputs,
    conditioning,
    w_mod,
    b_mod,
    w_qkv,
    b_qkv,
    w_out,
    b_out,
    w_fc1,
    b_fc1,
    w_fc2,
    b_fc2,
    cotangent,
):
    cond_act = jax.nn.silu(conditioning).astype(jnp.bfloat16)
    modulation_rows = modulate(cond_act, w_mod, b_mod)
    outcome = run_blocks(
        inputs, modulation_rows, w_qkv, b_qkv, w_out, b_out, w_fc1, b_fc1, w_fc2, b_fc2, cotangent
    )
    result, gradient_of_input, resid_parts, bfc1_part, bqkv_part, weight_grads = outcome
    dcond, totals = finish(
        conditioning, cond_act, w_mod, resid_parts, bfc1_part, bqkv_part, weight_grads
    )
    g_mod, g_bmod, g_qkv, g_bqkv, g_out, g_bout, g_fc1, g_bfc1, g_fc2, g_bfc2 = totals
    return (
        result,
        gradient_of_input,
        dcond,
        g_mod,
        g_bmod,
        g_qkv,
        g_bqkv,
        g_out,
        g_bout,
        g_fc1,
        g_bfc1,
        g_fc2,
        g_bfc2,
    )


def solution(mesh):
    by_latent = on_device_by_latent(mesh.shape["dp"])

    def body(*args):
        fits = fits_by_latent(mesh) and args[0].shape[0] % 2 == 0
        return by_latent(*args) if fits else on_device(*args)

    return jax.shard_map(
        body,
        mesh=mesh,
        in_specs=(
            P("dp", "col", "row"),
            P("dp", "col"),
            P("col", None, "row"),
            P(None, "row"),
            P("row", None, "col"),
            P(None, "col"),
            P("col", "row"),
            P("row"),
            P("row", "col"),
            P("col"),
            P("col", "row"),
            P("row"),
            P("dp", "col", "row"),
        ),
        out_specs=(
            P("dp", "col", "row"),
            P("dp", "col", "row"),
            P("dp", "col"),
            P("col", None, "row"),
            P(None, "row"),
            P("row", None, "col"),
            P(None, "col"),
            P("col", "row"),
            P("row"),
            P("row", "col"),
            P("col"),
            P("col", "row"),
            P("row"),
        ),
        check_vma=False,
    )
```
